256 devices in a mesh: seq: 64 (over y, z, core), grp: 4 (over x).
Axes of the slice: x: 4, y: 4, z: 8, core: 2. Of those that a mesh axis runs over, the one named last changes fastest.
Arguments:
- doc_lengths: int32 [4, 16], P('grp'), may hold values from 1 to 1024, 8192 in all within a row
- hidden: bfloat16 [4, 8192, 7168], P('grp', 'seq'), may hold values from -16 to 16
- gate_weight: bfloat16 [7168, 64], P(('seq', 'grp')), may hold values from -0.0625 to 0.0625
- target_query: bfloat16 [4, 8192, 36864], P('grp', 'seq'), may hold values from -30 to 30
- latent_keys: bfloat16 [4, 8192, 576], P('grp', 'seq'), may hold values from -6 to 6
- index_query: bfloat16 [4, 8192, 8192], P('grp', 'seq'), may hold values from -15 to 15
- index_keys: bfloat16 [4, 8192, 128], P('grp', 'seq'), may hold values from -6 to 6
Outputs:
- divergence: float32 [4, 8192], P('grp', 'seq')
- grad_gate: float32 [7168, 64], P(('seq', 'grp'))
The draws below stay inside these ranges and needn't reach their ends.
All inputs are finite; a program needn't handle non-finite values.
Results may differ from the reference program's by a relative error of at most 0.0022.
Values may be sent and summed in bfloat16 or wider, within the bound.
A program may use at most 128 MiB of HBM per device.

```python
import math
import jax
import jax.numpy as jnp
import numpy as np
from jax import lax

D = 7168
HI = 64
DI = 128
HT = 64
RK = 576
TOK_DEV = 128
GROUPS = 4
TOKG = 8192
DOC_MOST = 1024
WIN = 1152
DOCS = 16
N_SEQ = 64


def latent_base(key):
    return jnp.clip(jax.random.normal(jax.random.fold_in(key, 101), (GROUPS, TOKG, RK), jnp.float32), -6.0, 6.0)


def index_base(key):
    return jnp.clip(jax.random.normal(jax.random.fold_in(key, 201), (GROUPS, TOKG, DI), jnp.float32), -6.0, 6.0)


def draw_latent_keys(key, part):
    return latent_base(key).astype(jnp.bfloat16)


def draw_index_keys(key, part):
    return index_base(key).astype(jnp.bfloat16)


def draw_target_query(key, part):
    values = jnp.clip(jax.random.normal(jax.random.fold_in(key, 102), (GROUPS, TOKG, HT, RK), jnp.float32), -6.0, 6.0)
    return jnp.clip(values, -30.0, 30.0).reshape(GROUPS, TOKG, HT * RK).astype(jnp.bfloat16)


def draw_index_query(key, part):
    values = 0.5 * jnp.clip(jax.random.normal(jax.random.fold_in(key, 202), (GROUPS, TOKG, HI, DI), jnp.float32), -6.0, 6.0)
    return jnp.clip(values, -15.0, 15.0).reshape(GROUPS, TOKG, HI * DI).astype(jnp.bfloat16)


def with_spikes(array, rng, source, target, blocks, factor):
    def block_of(dim):
        return (jnp.arange(array.shape[dim]) // (array.shape[dim] // blocks)).reshape((-1,) + (1,) * (array.ndim - 1 - dim))

    one_side = jax.random.permutation(rng, blocks)[block_of(target)]
    second = (block_of(target) + blocks // 2) % blocks
    return jnp.where((block_of(source) == one_side) | (block_of(source) == second), factor * array, array)


def shard_levels(own_key, shape, split, low, high):
    loudness, own = 1.0, jax.random.fold_in(own_key, 6)
    for axis_at, blocks in split:
        steps = jnp.exp(jax.random.uniform(jax.random.fold_in(own, axis_at), (blocks,), jnp.float32, low / len(split), high / len(split)))
        loudness = loudness * jnp.repeat(steps, shape[axis_at] // blocks).reshape([-1 if axis == axis_at else 1 for axis in range(len(shape))])
    return loudness


def length_profile(number_of, total, most, slope):
    loads = [(1 << 20) // math.isqrt(standing ** slope) + 1 for standing in range(2, number_of + 1)]
    surplus, given = total - most - (number_of - 1), [1] * (number_of - 1)
    while surplus > 0:
        candidates = [i for i in range(number_of - 1) if given[i] < most]
        mass, left = sum([loads[i] for i in candidates]), surplus
        for i in candidates:
            extra = min(most - given[i], max(1, left * loads[i] // mass), surplus)
            given[i] = given[i] + extra
            surplus = surplus - extra
    return np.array([most] + given)


def ragged(stream_key, amount, total, bound, lean):
    if amount == 2:
        one = jax.random.randint(stream_key, (), max(1, total - bound), min(bound, total - 1) + 1)
        return jnp.stack([one, total - one])
    tallies = jnp.asarray(length_profile(amount, total, bound, lean), jnp.int32)
    couples = (amount - 1) // 2
    giver, sink = tallies[1:1 + 2 * couples:2], tallies[2:2 + 2 * couples:2]
    slack = jnp.minimum(giver - 1, bound - sink)
    moved = jax.random.randint(jax.random.fold_in(stream_key, 1), (couples,), 0, 1 << 20) % (slack + 1)
    tallies = tallies.at[1:1 + 2 * couples:2].set(giver - moved).at[2:2 + 2 * couples:2].set(sink + moved)
    return tallies[jax.random.permutation(jax.random.fold_in(stream_key, 2), amount)]


def normal_values(own_key, dims, scale, most, pieces=(), kind=jnp.bfloat16):
    entries = scale * jax.random.normal(own_key, dims, jnp.float32)
    if pieces:
        entries = entries * shard_levels(own_key, dims, pieces, -0.22, 0.18)
    return jnp.clip(entries, -most, most).astype(kind)


def gaussian_with(rng, dims, spread, bound, split, heavy, held_as=jnp.bfloat16):
    values = spread * jax.random.normal(rng, dims, jnp.float32)
    if split:
        values = values * shard_levels(rng, dims, split, -0.22, 0.18)
    return jnp.clip(with_spikes(values, jax.random.fold_in(rng, 3), *heavy), -bound, bound).astype(held_as)


def setup_inputs(seed: int = 0) -> dict:
    key_of = jax.random.split(jax.random.key(seed), 8)
    return {
        "doc_lengths": jax.vmap(lambda own: ragged(own, DOCS, TOKG, DOC_MOST, 2))(jax.random.split(key_of[0], GROUPS)).reshape((GROUPS, DOCS)).astype(jnp.int32),
        "hidden": gaussian_with(key_of[1], (GROUPS, TOKG, D), 1.0, 16.0, ((0, 4), (1, 64)), (1, 2, 64, 4.0)),
        "gate_weight": normal_values(key_of[2], (D, HI), D ** -0.5, 0.0625, ((0, 256),)),
        "target_query": draw_target_query(jax.random.fold_in(key_of[7], 71), 0),
        "latent_keys": draw_latent_keys(jax.random.fold_in(key_of[7], 71), 0),
        "index_query": draw_index_query(jax.random.fold_in(key_of[7], 71), 0),
        "index_keys": draw_index_keys(jax.random.fold_in(key_of[7], 71), 0),
    }


target_scale = 0.07216878364870322
highest = lax.Precision.HIGHEST


def divergence_terms(target_q, index_q, gate_values, latent_win, index_win, query_pos, key_pos, query_start):
    batch_n, row_n = query_pos.shape
    latent_projection_weight = latent_win.shape[-1]
    index_w = index_win.shape[-1]
    target_heads = target_q.reshape(batch_n, row_n, -1, latent_projection_weight).astype(jnp.float32)
    indexer_head_weights = index_q.reshape(batch_n, row_n, -1, index_w).astype(jnp.float32)
    allowed = (key_pos[:, None, :] >= query_start[:, :, None]) & (key_pos[:, None, :] <= query_pos[:, :, None])
    logits = jnp.einsum("srhc,skc->srhk", target_heads, latent_win.astype(jnp.float32), precision=highest) * target_scale
    logits = jnp.where(allowed[:, :, None, :], logits, -jnp.inf)
    peak_value = jnp.max(logits, axis=-1, keepdims=True)
    exponent = jnp.exp(logits - peak_value)
    probabilities = exponent / jnp.sum(exponent, axis=-1, keepdims=True)
    target = jnp.mean(probabilities, axis=2)
    relu_score = jnp.maximum(jnp.einsum("srhd,skd->srhk", indexer_head_weights, index_win.astype(jnp.float32), precision=highest), 0.0)
    factor = index_w ** -0.5
    score = factor * jnp.einsum("srh,srhk->srk", gate_values, relu_score, precision=highest)
    masked = jnp.where(allowed, score, -jnp.inf)
    largest_value_seen = jnp.max(masked, axis=-1, keepdims=True)
    shifted = masked - largest_value_seen
    log_model = shifted - jnp.log(jnp.sum(jnp.exp(shifted), axis=-1, keepdims=True))
    log_model = jnp.where(allowed, log_model, 0.0)
    model_prob = jnp.where(allowed, jnp.exp(log_model), 0.0)
    positive = target > 0
    target_log_probabilities = jnp.where(positive, target * jnp.log(jnp.where(positive, target, 1.0)), 0.0)
    row_div = jnp.sum(jnp.where(allowed, target_log_probabilities - target * log_model, 0.0), axis=-1)
    delta_terms = factor * jnp.einsum("srk,srhk->srh", model_prob - target, relu_score, precision=highest)
    return row_div, delta_terms


def reference(doc_lengths, hidden, gate_weight, target_query, latent_keys, index_query, index_keys):
    outputs = []
    grad_total = jnp.zeros((D, HI), jnp.float32)
    for group_index in range(GROUPS):
        lengths = doc_lengths[group_index]
        doc_ends = jnp.cumsum(lengths)
        gates_all = jnp.dot(hidden[group_index], gate_weight, preferred_element_type=jnp.float32)
        latent_padding_rows = jnp.concatenate([jnp.zeros((DOC_MOST, RK), latent_keys.dtype), latent_keys[group_index]], 0)
        index_pad = jnp.concatenate([jnp.zeros((DOC_MOST, DI), index_keys.dtype), index_keys[group_index]], 0)
        target_group = target_query[group_index]
        index_group = index_query[group_index]

        def home_block(block_index):
            low_row = (block_index * TOK_DEV).astype(jnp.int32)
            query_pos = (low_row + jnp.arange(TOK_DEV, dtype=jnp.int32)).astype(jnp.int32)
            key_pos = (low_row - DOC_MOST + jnp.arange(WIN, dtype=jnp.int32)).astype(jnp.int32)
            query_start = jnp.sum(lengths[None, :] * (doc_ends[None, :] <= query_pos[:, None]).astype(jnp.int32), -1).astype(jnp.int32)
            target_rows = lax.dynamic_slice_in_dim(target_group, low_row, TOK_DEV, 0)
            index_rows = lax.dynamic_slice_in_dim(index_group, low_row, TOK_DEV, 0)
            gate_rows = lax.dynamic_slice_in_dim(gates_all, low_row, TOK_DEV, 0)
            latent_win = lax.dynamic_slice_in_dim(latent_padding_rows, low_row, WIN, 0)
            index_win = lax.dynamic_slice_in_dim(index_pad, low_row, WIN, 0)
            row_div, delta_terms = divergence_terms(target_rows[None], index_rows[None], gate_rows[None], latent_win[None], index_win[None], query_pos[None], key_pos[None], query_start[None])
            return row_div[0], delta_terms[0]

        row_div, delta_terms = lax.map(home_block, jnp.arange(N_SEQ, dtype=jnp.int32))
        outputs.append(row_div.reshape(TOKG))
        gate_delta = (delta_terms.reshape(TOKG, HI) / TOK_DEV).astype(jnp.bfloat16)
        grad_total = grad_total + jnp.dot(hidden[group_index].T, gate_delta, preferred_element_type=jnp.float32)
    return jnp.stack(outputs, 0), grad_total
```

```python
import functools
import math

import jax
import jax.numpy as jnp
from jax import lax
from jax.experimental import pallas as pl
from jax.experimental.pallas import tpu as pltpu
from jax.sharding import Mesh
from jax.sharding import PartitionSpec as P

SEQ = ("seq_0", "seq_1", "seq_2")
SEQ_GRP = ("seq_0", "seq_1", "seq_2", "grp")
MESH = pl.DeviceIdType.MESH

ROWS = 128
HEADS = 64
LAT = 576
DI = 128
WIN = 1152
LOOK = 1024
D = 7168
DOCS = 16
PAIR = 2 * LAT
CUT = 640
DEEP = 768
UNIT = 4 * ROWS
SLOTS = 4
NEG = -1e30
TARGET_SCALE = 0.07216878364870322
EXP_SCALE = TARGET_SCALE * math.log2(math.e)
BF = jnp.bfloat16
F32 = jnp.float32
VMEM_MOST = 67_043_328


def compute_kernel(
    lens_ref, q_hbm, iq_hbm, hid_hbm, lat_hbm, ik_hbm, w_hbm,
    div_ref, part_ref,
    ke, ko, ikt, qbuf, rel_a, rel_b, acc, score, dif, gates3, hid, ht, iq, lat, ik, wf, gd,
    qsem, isem,
):
    seq = (lax.axis_index("seq_0") * 8 + lax.axis_index("seq_1")) * 2 + lax.axis_index("seq_2")
    first = lax.axis_index("seq_2") * ROWS

    def q_copy(unit, slot):
        quad, parity = unit // 2, unit % 2
        return [
            pltpu.make_async_copy(
                q_hbm.at[:, pl.ds(pl.multiple_of((quad * 4 + k) * PAIR + parity * (PAIR - CUT), 128), CUT)],
                qbuf.at[slot, pl.ds(k * ROWS, ROWS), pl.ds(0, CUT)],
                qsem.at[slot, k],
            )
            for k in range(4)
        ]

    lat_in = pltpu.make_async_copy(lat_hbm, lat, isem.at[0])
    ik_in = pltpu.make_async_copy(ik_hbm, ik, isem.at[1])
    lat_in.start()
    ik_in.start()
    for s in range(SLOTS):
        for c in q_copy(s, s):
            c.start()
    iq_in = pltpu.make_async_copy(iq_hbm, iq, isem.at[2])
    hid_in = pltpu.make_async_copy(hid_hbm, hid, isem.at[3])
    w_in = pltpu.make_async_copy(w_hbm, wf, isem.at[4])
    iq_in.start()
    hid_in.start()
    w_in.start()

    row = lax.broadcasted_iota(jnp.int32, (ROWS, ROWS), 0)
    lane = lax.broadcasted_iota(jnp.int32, (ROWS, ROWS), 1)
    pos = seq * ROWS + row
    start = jnp.zeros((ROWS, ROWS), jnp.int32)
    end = jnp.int32(0)
    for k in range(DOCS):
        length = lens_ref[0, k]
        end = end + length
        start = start + jnp.where(pos >= end, length, 0)
    eye = jnp.where(row == lane, 1.0, 0.0).astype(BF)
    for s in range(SLOTS):
        for k in range(4):
            qbuf[s, k * ROWS : (k + 1) * ROWS, CUT:DEEP] = eye
    for t in range(WIN // ROWS):
        key = seq * ROWS - LOOK + t * ROWS + lane
        bias = jnp.where(jnp.logical_and(key >= start, key <= pos), 0.0, NEG).astype(BF)
        ke[CUT:DEEP, t * ROWS : (t + 1) * ROWS] = bias
        ko[CUT:DEEP, t * ROWS : (t + 1) * ROWS] = bias
    ke[LAT:CUT, :] = jnp.zeros((CUT - LAT, WIN), BF)
    ko[0 : CUT - LAT, :] = jnp.zeros((CUT - LAT, WIN), BF)
    acc[...] = jnp.zeros((ROWS, WIN), F32)

    lat_in.wait()
    for t in range(WIN // ROWS):
        rows = pl.ds(pl.multiple_of(first + t * ROWS, ROWS), ROWS)
        cols = slice(t * ROWS, (t + 1) * ROWS)
        block = lat[rows, :].T
        ke[0:LAT, cols] = block
        ko[CUT - LAT : CUT, cols] = block
    ik_in.wait()
    for t in range(WIN // ROWS):
        rows = pl.ds(pl.multiple_of(first + t * ROWS, ROWS), ROWS)
        ikt[:, t * ROWS : (t + 1) * ROWS] = ik[rows, :].T

    s_even, s_odd = rel_a.at[0], rel_b.at[0]

    def logits(slot, keys, dest):
        dest[...] = jnp.dot(qbuf[slot], keys[...], preferred_element_type=F32)

    def heads_sum(src):
        for g in range(ROWS // 8):
            rows = slice(8 * g, 8 * g + 8)
            total = acc[rows, :]
            for k in range(4):
                s = src[k * ROWS + 8 * g : k * ROWS + 8 * g + 8, :]
                top = jnp.max(s, axis=1, keepdims=True)
                p = jnp.exp2((s - top) * EXP_SCALE)
                total = total + p * (1.0 / jnp.sum(p, axis=1, keepdims=True))
            acc[rows, :] = total

    def wait_q(unit, slot):
        for c in q_copy(unit, slot):
            c.wait()

    def next_q(unit, slot):
        @pl.when(unit + SLOTS < 16)
        def _():
            for c in q_copy(unit + SLOTS, slot):
                c.start()

    wait_q(0, 0)
    logits(0, ke, s_even)
    next_q(0, 0)

    def pair_step(i, _):
        odd, even = 2 * i + 1, 2 * i + 2
        wait_q(odd, odd % SLOTS)
        logits(odd % SLOTS, ko, s_odd)
        heads_sum(s_even)
        next_q(odd, odd % SLOTS)

        @pl.when(even < 16)
        def _():
            wait_q(even, even % SLOTS)

        logits(even % SLOTS, ke, s_even)
        heads_sum(s_odd)
        next_q(even, even % SLOTS)
        return 0

    lax.fori_loop(0, 8, pair_step, 0)

    hid_in.wait()
    w_in.wait()
    gates = jnp.dot(hid[...], wf[...], preferred_element_type=F32)
    for h in range(HEADS):
        gates3[h] = jnp.broadcast_to(gates[:, h : h + 1], (ROWS, ROWS))
    iq_in.wait()
    score[...] = jnp.zeros((ROWS, WIN), F32)

    def relus(unit, dest):
        q4 = jnp.concatenate(
            [iq[:, pl.ds(pl.multiple_of((unit * 4 + k) * DI, DI), DI)] for k in range(4)], axis=0
        )
        dest[...] = jnp.dot(q4, ikt[...], preferred_element_type=F32)

    def score_sum(unit, src):
        for g in range(ROWS // 8):
            rows = slice(8 * g, 8 * g + 8)
            tiles = [score[rows, t * 128 : t * 128 + 128] for t in range(9)]
            for k in range(4):
                gate = gates3[unit * 4 + k, rows, :]
                for t in range(9):
                    s = src[k * ROWS + 8 * g : k * ROWS + 8 * g + 8, t * 128 : t * 128 + 128]
                    tiles[t] = tiles[t] + gate * jnp.maximum(s, 0.0)
            for t in range(9):
                score[rows, t * 128 : t * 128 + 128] = tiles[t]

    relus(0, rel_a.at[0])

    def score_step(i, _):
        relus(2 * i + 1, rel_b.at[i])
        score_sum(2 * i, rel_a.at[i])
        nxt = jnp.minimum(i + 1, 7)
        relus(2 * nxt, rel_a.at[nxt])
        score_sum(2 * i + 1, rel_b.at[i])
        return 0

    lax.fori_loop(0, 8, score_step, 0)

    factor = DI**-0.5
    for g in range(ROWS // 8):
        rows = slice(8 * g, 8 * g + 8)
        bias = ke[CUT + 16 * (g // 2) : CUT + 16 * (g // 2) + 16, :].astype(F32)[8 * (g % 2) : 8 * (g % 2) + 8, :]
        allowed = bias == 0.0
        sc = jnp.where(allowed, score[rows, :] * factor, NEG)
        shifted = sc - jnp.max(sc, axis=1, keepdims=True)
        log_model = shifted - jnp.log(jnp.sum(jnp.exp(shifted), axis=1, keepdims=True))
        model = jnp.exp(log_model)
        target = acc[rows, :] * (1.0 / HEADS)
        positive = target > 0.0
        terms = jnp.where(positive, target * (jnp.log(jnp.where(positive, target, 1.0)) - log_model), 0.0)
        terms = jnp.where(allowed, terms, 0.0)
        div_ref[rows, :] = jnp.broadcast_to(jnp.sum(terms, axis=1, keepdims=True), (8, 128))
        dif[rows, :] = jnp.where(allowed, model - target, 0.0)

    gd[...] = jnp.zeros((ROWS, ROWS), F32)
    lane8 = lax.broadcasted_iota(jnp.int32, (8, ROWS), 1)

    def delta_sum(unit, src):
        for g in range(ROWS // 8):
            rows = slice(8 * g, 8 * g + 8)
            out = gd[rows, :]
            tiles = [dif[rows, t * 128 : t * 128 + 128] for t in range(9)]
            for k in range(4):
                total = None
                for t in range(9):
                    s = src[k * ROWS + 8 * g : k * ROWS + 8 * g + 8, t * 128 : t * 128 + 128]
                    term = tiles[t] * jnp.maximum(s, 0.0)
                    total = term if total is None else total + term
                value = jnp.sum(total, axis=1, keepdims=True)
                out = jnp.where(lane8 == unit * 4 + k, value, out)
            gd[rows, :] = out

    def delta_step(i, _):
        delta_sum(2 * i, rel_a.at[i])
        delta_sum(2 * i + 1, rel_b.at[i])
        return 0

    for t in range(D // 128):
        ht[t * 128 : t * 128 + 128, :] = hid[:, t * 128 : t * 128 + 128].T
    lax.fori_loop(0, 8, delta_step, 0)

    delta = (gd[...] * factor / ROWS).astype(BF).astype(F32)
    two = jnp.concatenate([delta, pltpu.roll(delta, 64, 1)], axis=0).astype(BF)

    def part_step(i, _):
        lo = pl.ds(pl.multiple_of(i * 224, 16), 112)
        hi = pl.ds(pl.multiple_of(i * 224 + 112, 16), 112)
        both = jnp.concatenate([ht[lo, :], ht[hi, :]], axis=1)
        out = jnp.dot(both, two, preferred_element_type=F32)
        pad = jnp.zeros((2, 128), F32)
        for x in range(4):
            for half in range(2):
                at = x * 28 + half * 14
                part_ref[half, x, i // 8, i % 8] = jnp.concatenate([out[at : at + 14, :], pad], axis=0)
        return 0

    lax.fori_loop(0, 32, part_step, 0)


def compute(lens, q, iq, hid, lat, ik, w):
    hbm = pl.BlockSpec(memory_space=pl.ANY)
    vmem = pl.BlockSpec(memory_space=pltpu.VMEM)
    return pl.pallas_call(
        compute_kernel,
        out_shape=(
            jax.ShapeDtypeStruct((ROWS, 128), F32),
            jax.ShapeDtypeStruct((2, 4, 4, 8, 16, 128), F32),
        ),
        in_specs=[pl.BlockSpec(memory_space=pltpu.SMEM)] + [hbm] * 6,
        out_specs=(vmem, vmem),
        scratch_shapes=[
            pltpu.VMEM((DEEP, WIN), BF),
            pltpu.VMEM((DEEP, WIN), BF),
            pltpu.VMEM((DI, WIN), BF),
            pltpu.VMEM((SLOTS, UNIT, DEEP), BF),
            pltpu.VMEM((8, UNIT, WIN), F32),
            pltpu.VMEM((8, UNIT, WIN), F32),
            pltpu.VMEM((ROWS, WIN), F32),
            pltpu.VMEM((ROWS, WIN), F32),
            pltpu.VMEM((ROWS, WIN), F32),
            pltpu.VMEM((HEADS, ROWS, ROWS), F32),
            pltpu.VMEM((ROWS, D), BF),
            pltpu.VMEM((D, ROWS), BF),
            pltpu.VMEM((ROWS, HEADS * DI), BF),
            pltpu.VMEM((WIN + ROWS, LAT), BF),
            pltpu.VMEM((WIN + ROWS, DI), BF),
            pltpu.VMEM((D, HEADS), BF),
            pltpu.VMEM((ROWS, ROWS), F32),
            pltpu.SemaphoreType.DMA((SLOTS, 4)),
            pltpu.SemaphoreType.DMA((5,)),
        ],
        compiler_params=pltpu.CompilerParams(vmem_limit_bytes=VMEM_MOST),
        cost_estimate=pl.CostEstimate(flops=20_000_000_000, bytes_accessed=18_000_000, transcendentals=9_400_000),
    )(lens, q, iq, hid, lat, ik, w)


def sync_with(peers):
    barrier = pltpu.get_barrier_semaphore()
    for peer in peers:
        pl.semaphore_signal(barrier, inc=1, device_id=peer, device_id_type=MESH)
    pl.semaphore_wait(barrier, len(peers))


def chip_after(y, z):
    return {"seq_0": lax.rem(y + (z + 1) // 8, 4), "seq_1": lax.rem(z + 1, 8)}


def chip_before(y, z):
    return {"seq_0": lax.rem(y + 3 + (z + 7) // 8, 4), "seq_1": lax.rem(z + 7, 8)}


def fetch_kernel(
    lat_ref, ik_ref, gw_ref, lat_out, ik_out, w_out,
    wx, wcat, wb, ring_s, ring_r, side_s, side_r, w_s, w_r,
):
    y, z, core, x = (lax.axis_index(a) for a in SEQ_GRP)
    ahead, behind = chip_after(y, z), chip_before(y, z)
    partner = {"seq_2": 1 - core}
    xs = [{"grp": lax.rem(x + d, 4)} for d in range(1, 4)]
    ys = [{"seq_0": lax.rem(y + d, 4)} for d in range(1, 4)]
    zs = [{"seq_1": lax.rem(z + d, 8)} for d in range(1, 8)]
    sync_with([partner] + xs + ys + zs + [ahead, behind])

    def remote(src, dst, send, recv, peer):
        return pltpu.make_async_remote_copy(
            src_ref=src, dst_ref=dst, send_sem=send, recv_sem=recv, device_id=peer, device_id_type=MESH
        )

    def slot(k):
        return pl.ds(pl.multiple_of((8 - 2 * k + core) * ROWS, ROWS), ROWS)

    wx[x] = gw_ref[...]
    x_copies = []
    for d in range(1, 4):
        c = remote(gw_ref, wx.at[x], w_s.at[d], w_r.at[d], xs[d - 1])
        c.start()
        x_copies.append(c)

    def ring(k, src_lat, src_ik):
        return [
            remote(src_ik, ik_out.at[slot(k + 1)], ring_s.at[k, 0], ring_r.at[k, 0], ahead),
            remote(src_lat, lat_out.at[slot(k + 1)], ring_s.at[k, 1], ring_r.at[k, 1], ahead),
        ]

    def side(k, src_lat, src_ik):
        return [
            remote(src_ik, ik_out.at[slot(k)], side_s.at[k, 0], side_r.at[k, 0], partner),
            remote(src_lat, lat_out.at[slot(k)], side_s.at[k, 1], side_r.at[k, 1], partner),
        ]

    hop = ring(0, lat_ref, ik_ref)
    for c in hop:
        c.start()
    sides = [side(0, lat_ref, ik_ref)]
    for c in sides[0]:
        c.start()
    lat_out[slot(0), :] = lat_ref[...]
    ik_out[slot(0), :] = ik_ref[...]

    for c in x_copies:
        c.wait()
    for j in range(4):
        wcat[28 * j : 28 * j + 28, :] = wx[j].astype(F32)
    wb[core, y, z] = wcat[...].astype(BF)
    z_copies = []
    for d in range(1, 8):
        c = remote(wb.at[core, y, z], wb.at[core, y, z], w_s.at[3 + d], w_r.at[3 + d], zs[d - 1])
        c.start()
        z_copies.append(c)

    for k in range(1, 5):
        for c in hop:
            c.wait()
        here_lat, here_ik = lat_out.at[slot(k)], ik_out.at[slot(k)]
        if k < 4:
            hop = ring(k, here_lat, here_ik)
            for c in hop:
                c.start()
        sides.append(side(k, here_lat, here_ik))
        for c in sides[-1]:
            c.start()
        if k == 1:
            for c in z_copies:
                c.wait()
            y_copies = []
            for d in range(1, 4):
                c = remote(wb.at[core, y], wb.at[core, y], w_s.at[10 + d], w_r.at[10 + d], ys[d - 1])
                c.start()
                y_copies.append(c)
        if k == 3:
            for c in y_copies:
                c.wait()
            last = remote(wb.at[core], wb.at[core], w_s.at[0], w_r.at[0], partner)
            last.start()
    last.wait()
    for yy in range(4):
        for zz in range(8):
            for cc in range(2):
                at = ((yy * 8 + zz) * 2 + cc) * 112
                w_out[at : at + 112, :] = wb[cc, yy, zz]
    for pair in sides:
        for c in pair:
            c.wait()


def fetch(lat, ik, gw):
    vmem = pl.BlockSpec(memory_space=pltpu.VMEM)
    return pl.pallas_call(
        fetch_kernel,
        out_shape=(
            jax.ShapeDtypeStruct((WIN + ROWS, LAT), BF),
            jax.ShapeDtypeStruct((WIN + ROWS, DI), BF),
            jax.ShapeDtypeStruct((D, HEADS), BF),
        ),
        in_specs=[vmem] * 3,
        out_specs=(vmem,) * 3,
        scratch_shapes=[
            pltpu.VMEM((4, 28, HEADS), BF),
            pltpu.VMEM((112, HEADS), F32),
            pltpu.VMEM((2, 4, 8, 112, HEADS), BF),
            pltpu.SemaphoreType.DMA((4, 2)),
            pltpu.SemaphoreType.DMA((4, 2)),
            pltpu.SemaphoreType.DMA((5, 2)),
            pltpu.SemaphoreType.DMA((5, 2)),
            pltpu.SemaphoreType.DMA((14,)),
            pltpu.SemaphoreType.DMA((14,)),
        ],
        compiler_params=pltpu.CompilerParams(collective_id=0, has_side_effects=True, vmem_limit_bytes=VMEM_MOST),
    )(lat, ik, gw)


def reduce_kernel(part_ref, out_ref, rc, s1, rx, s2, ry, s3, rz, s4, fin, ssem, rsem):
    y, z, core, x = (lax.axis_index(a) for a in SEQ_GRP)
    partner = {"seq_2": 1 - core}
    xs = [{"grp": lax.rem(x + d, 4)} for d in range(1, 4)]
    ys = [{"seq_0": lax.rem(y + d, 4)} for d in range(1, 4)]
    zs = [{"seq_1": lax.rem(z + d, 8)} for d in range(1, 8)]
    sync_with([partner] + xs + ys + zs)

    def remote(src, dst, sem, peer):
        return pltpu.make_async_remote_copy(
            src_ref=src, dst_ref=dst, send_sem=ssem.at[sem], recv_sem=rsem.at[sem],
            device_id=peer, device_id_type=MESH,
        )

    def exchange(copies):
        for c in copies:
            c.start()
        for c in copies:
            c.wait()

    exchange([remote(part_ref.at[1 - core, k], rc.at[k], k, partner) for k in range(4)])
    for k in range(4):
        s1[k] = part_ref[core, k] + rc[k]
    exchange([remote(s1.at[lax.rem(x + d, 4)], rx.at[d - 1], 3 + d, xs[d - 1]) for d in range(1, 4)])
    s2[...] = s1[x] + rx[0] + rx[1] + rx[2]
    exchange([remote(s2.at[lax.rem(y + d, 4)], ry.at[d - 1], 6 + d, ys[d - 1]) for d in range(1, 4)])
    s3[...] = s2[y] + ry[0] + ry[1] + ry[2]
    exchange([remote(s3.at[lax.rem(z + d, 8)], rz.at[d - 1], 9 + d, zs[d - 1]) for d in range(1, 8)])
    total = s3[z]
    for d in range(7):
        total = total + rz[d]
    s4[...] = total
    exchange([remote(s4, fin, 17, partner)])
    low = jnp.where(core == 0, s4[...], fin[...])
    high = jnp.where(core == 0, fin[...], s4[...])
    full = jnp.concatenate([low[0:14, :], high[0:14, :]], axis=0)
    out_ref[...] = jnp.where(core == 0, full[:, 0:64], full[:, 64:128])


def reduce_all(part):
    vmem = pl.BlockSpec(memory_space=pltpu.VMEM)
    return pl.pallas_call(
        reduce_kernel,
        out_shape=jax.ShapeDtypeStruct((28, HEADS), F32),
        in_specs=[vmem],
        out_specs=vmem,
        scratch_shapes=[
            pltpu.VMEM((4, 4, 8, 16, 128), F32),
            pltpu.VMEM((4, 4, 8, 16, 128), F32),
            pltpu.VMEM((3, 4, 8, 16, 128), F32),
            pltpu.VMEM((4, 8, 16, 128), F32),
            pltpu.VMEM((3, 8, 16, 128), F32),
            pltpu.VMEM((8, 16, 128), F32),
            pltpu.VMEM((7, 16, 128), F32),
            pltpu.VMEM((16, 128), F32),
            pltpu.VMEM((16, 128), F32),
            pltpu.SemaphoreType.DMA((18,)),
            pltpu.SemaphoreType.DMA((18,)),
        ],
        compiler_params=pltpu.CompilerParams(collective_id=1, has_side_effects=True),
    )(part)


def body(doc_lengths, hidden, gate_weight, target_query, latent_keys, index_query, index_keys):
    lat, ik, w = fetch(latent_keys[0], index_keys[0], gate_weight)
    div, part = compute(doc_lengths, target_query[0], index_query[0], hidden[0], lat, ik, w)
    return div[:, 0].reshape(1, ROWS), reduce_all(part)


def solution(mesh):
    split = Mesh(mesh.devices.reshape(4, 8, 2, mesh.shape["grp"]), SEQ_GRP)
    rows = P("grp", SEQ, None)
    in_specs = (P("grp", None), rows, P(SEQ_GRP, None), rows, rows, rows, rows)
    out_specs = (P("grp", SEQ), P(SEQ_GRP, None))
    return jax.shard_map(body, mesh=split, in_specs=in_specs, out_specs=out_specs, check_vma=False)
```

```python
import math

import jax
import jax.numpy as jnp
from jax import lax
from jax.experimental import pallas as pl
from jax.experimental.pallas import tpu as pltpu
from jax.sharding import Mesh
from jax.sharding import PartitionSpec as P

SEQ = ("seq_0", "seq_1", "seq_2")
SEQ_GRP = ("seq_0", "seq_1", "seq_2", "grp")
MESH = pl.DeviceIdType.MESH

ROWS = 128
HEADS = 64
LAT = 576
DI = 128
WIN = 1152
LOOK = 1024
D = 7168
DOCS = 16
PAIR = 2 * LAT
CUT = 640
DEEP = 768
PANEL = WIN + ROWS
QUARTER = D // 4
UNIT = 4 * ROWS
SLOTS = 4
NEG = -1e30
TARGET_SCALE = 0.07216878364870322
EXP_SCALE = TARGET_SCALE * math.log2(math.e)
BF = jnp.bfloat16
F32 = jnp.float32
VMEM_MOST = 67_043_328


def sync_with(peers):
    barrier = pltpu.get_barrier_semaphore()
    for peer in peers:
        pl.semaphore_signal(barrier, inc=1, device_id=peer, device_id_type=MESH)
    pl.semaphore_wait(barrier, len(peers))


def chip_after(y, z):
    return {"seq_0": lax.rem(y + (z + 1) // 8, 4), "seq_1": lax.rem(z + 1, 8)}


def chip_before(y, z):
    return {"seq_0": lax.rem(y + 3 + (z + 7) // 8, 4), "seq_1": lax.rem(z + 7, 8)}


def kernel(
    lens_ref, q_hbm, iq_hbm, hid_hbm, lat_hbm, ik_hbm, gw_ref,
    div_ref, out_ref,
    ke, ko, ikt, qbuf, rel_a, rel_b, acc, score, dif, starts, divs, gates, hid, lat, ik, gd,
    wx, wcat, wb, hy, ht, gall, part, rc, s1, rx, s2, rz, s3, fin,
    qsem, isem, ring_s, ring_r, side_s, side_r, w_s, w_r, t_s, t_r,
):
    y, z, core, x = (lax.axis_index(a) for a in SEQ_GRP)
    chip = y * 8 + z
    seq = chip * 2 + core
    window = pl.ds(pl.multiple_of(core * ROWS, ROWS), WIN)
    ahead, behind = chip_after(y, z), chip_before(y, z)
    partner = {"seq_2": 1 - core}
    xs = [{"grp": lax.rem(x + d, 4)} for d in range(1, 4)]
    ys = [{"seq_0": lax.rem(y + d, 4)} for d in range(1, 4)]
    zs = [{"seq_1": lax.rem(z + d, 8)} for d in range(1, 8)]

    def local(src, dst, sem):
        return pltpu.make_async_copy(src, dst, sem)

    def remote(src, dst, send, recv, peer):
        return pltpu.make_async_remote_copy(
            src_ref=src, dst_ref=dst, send_sem=send, recv_sem=recv, device_id=peer, device_id_type=MESH
        )

    def slot(k):
        return 8 - 2 * k + core

    def slot_rows(k):
        return pl.ds(pl.multiple_of((8 - 2 * k + core) * ROWS, ROWS), ROWS)

    def q_copy(unit, slot):
        quad, parity = unit // 2, unit % 2
        return [
            local(
                q_hbm.at[:, pl.ds(pl.multiple_of((quad * 4 + k) * PAIR + parity * (PAIR - CUT), 128), CUT)],
                qbuf.at[slot, pl.ds(k * ROWS, ROWS), pl.ds(0, CUT)],
                qsem.at[slot, k],
            )
            for k in range(4)
        ]

    own_lat = local(lat_hbm, lat.at[slot(0)], isem.at[0])
    own_ik = local(ik_hbm, ik.at[slot_rows(0)], isem.at[1])
    own_lat.start()
    own_ik.start()
    for u in range(SLOTS):
        for c in q_copy(u, u):
            c.start()
    sync_with([partner] + xs + ys + zs + [ahead, behind])

    def ring(k):
        src_lat, src_ik = (lat_hbm, ik_hbm) if k == 0 else (lat.at[slot(k)], ik.at[slot_rows(k)])
        return [
            remote(src_lat, lat.at[slot(k + 1)], ring_s.at[k, 0], ring_r.at[k, 0], ahead),
            remote(src_ik, ik.at[slot_rows(k + 1)], ring_s.at[k, 1], ring_r.at[k, 1], ahead),
        ]

    def side(k):
        src_lat, src_ik = (lat_hbm, ik_hbm) if k == 0 else (lat.at[slot(k)], ik.at[slot_rows(k)])
        return [
            remote(src_lat, lat.at[slot(k)], side_s.at[k, 0], side_r.at[k, 0], partner),
            remote(src_ik, ik.at[slot_rows(k)], side_s.at[k, 1], side_r.at[k, 1], partner),
        ]

    hop = ring(0)
    for c in hop:
        c.start()
    beside = side(0)
    for c in beside:
        c.start()
    wx[x] = gw_ref[...]
    w_copies = [remote(gw_ref, wx.at[x], w_s.at[d], w_r.at[d], xs[d - 1]) for d in range(1, 4)]
    for c in w_copies:
        c.start()
    hid_in = local(hid_hbm, hid, isem.at[3])
    own_quarter = local(hid_hbm.at[:, pl.ds(pl.multiple_of(y * QUARTER, 128), QUARTER)], hy.at[y], isem.at[4])
    hid_in.start()
    own_quarter.start()

    row = lax.broadcasted_iota(jnp.int32, (ROWS, ROWS), 0)
    lane = lax.broadcasted_iota(jnp.int32, (ROWS, ROWS), 1)
    pos = seq * ROWS + row
    start = jnp.zeros((ROWS, ROWS), jnp.int32)
    end = jnp.int32(0)
    for k in range(DOCS):
        length = lens_ref[0, k]
        end = end + length
        start = start + jnp.where(pos >= end, length, 0)
    starts[...] = start
    eye = jnp.where(row == lane, 1.0, 0.0).astype(BF)
    for u in range(SLOTS):
        for k in range(4):
            qbuf[u, k * ROWS : (k + 1) * ROWS, CUT:DEEP] = eye
    ke[LAT:CUT, :] = jnp.zeros((CUT - LAT, 2 * ROWS), BF)
    ko[0 : CUT - LAT, :] = jnp.zeros((CUT - LAT, 2 * ROWS), BF)
    acc[...] = jnp.zeros((ROWS, WIN), F32)
    score[...] = jnp.zeros((ROWS, WIN), F32)
    gd[...] = jnp.zeros((ROWS, ROWS), F32)
    gates[...] = jnp.zeros((ROWS, ROWS), F32)
    own_lat.wait()
    own_ik.wait()

    def keys_of(k):
        for j in range(2):
            at = (8 - 2 * k + j) * ROWS
            cols = slice(j * ROWS, (j + 1) * ROWS)
            key = (chip * 2 - 8 + 8 - 2 * k + j) * ROWS + lane
            own_start = starts[...]
            bias = jnp.where(jnp.logical_and(key >= own_start, key <= pos), 0.0, NEG).astype(BF)
            ke[CUT:DEEP, cols] = bias
            ko[CUT:DEEP, cols] = bias
            ke[0:LAT, cols] = lat[8 - 2 * k + j]
            ko[CUT - LAT : CUT, cols] = lat[8 - 2 * k + j]
            ikt[:, at : at + ROWS] = ik[at : at + ROWS, :].T

    for k in range(5):
        if k:
            for c in hop:
                c.wait()
            if k < 4:
                hop = ring(k)
                for c in hop:
                    c.start()
            beside = side(k)
            for c in beside:
                c.start()
        if k == 1:
            for c in w_copies:
                c.wait()
            for j in range(4):
                wcat[28 * j : 28 * j + 28, :] = wx[j].astype(F32)
            wb[y, z, core] = wcat[...].astype(BF)
            w_copies = [
                remote(wb.at[y, z, core], wb.at[y, z, core], w_s.at[3 + d], w_r.at[3 + d], zs[d - 1])
                for d in range(1, 8)
            ]
        if k == 2:
            for c in w_copies:
                c.wait()
            w_copies = [
                remote(wb.at[y, :, core], wb.at[y, :, core], w_s.at[10 + d], w_r.at[10 + d], ys[d - 1])
                for d in range(1, 4)
            ]
        if k == 4:
            for c in w_copies:
                c.wait()
            w_copies = [remote(wb.at[:, :, core], wb.at[:, :, core], w_s.at[0], w_r.at[0], partner)]
            h_copies = [
                remote(
                    hid_hbm.at[:, pl.ds(pl.multiple_of(lax.rem(y + d, 4) * QUARTER, 128), QUARTER)],
                    hy.at[y], w_s.at[13 + d], w_r.at[13 + d], ys[d - 1],
                )
                for d in range(1, 4)
            ]
        if k in (1, 2, 4):
            for c in w_copies:
                c.start()
        if k == 4:
            for c in h_copies:
                c.start()
        for c in beside:
            c.wait()
        keys_of(k)
        cols = slice((8 - 2 * k) * ROWS, (10 - 2 * k) * ROWS)

        def units(i, _, cols=cols, k=k):
            for parity, keys, store in ((0, ke, rel_a), (1, ko, rel_b)):
                unit = 2 * i + parity
                slot = unit % SLOTS
                for c in q_copy(unit, slot):
                    c.wait()
                store[i, :, cols] = jnp.dot(qbuf[slot], keys[...], preferred_element_type=F32)
                if k < 4:
                    for c in q_copy((unit + SLOTS) % 16, slot):
                        c.start()
                else:

                    @pl.when(unit + SLOTS < 16)
                    def _():
                        for c in q_copy(unit + SLOTS, slot):
                            c.start()

            return 0

        lax.fori_loop(0, 8, units, 0)

    iq_copies = [
        local(
            iq_hbm.at[:, pl.ds(u * 4 * DI, 4 * DI)],
            qbuf.at[u // 4, pl.ds(u % 4 * ROWS, ROWS), pl.ds(0, 4 * DI)],
            qsem.at[u // 4, u % 4],
        )
        for u in range(16)
    ]
    for c in iq_copies:
        c.start()
    for c in w_copies:
        c.wait()

    hid_in.wait()
    gates[:, 0:HEADS] = jnp.dot(hid[...], wb[...].reshape(D, HEADS), preferred_element_type=F32)
    for c in iq_copies:
        c.wait()

    def heads_sum(src):
        for g in range(ROWS // 8):
            rows = slice(8 * g, 8 * g + 8)
            total = acc[rows, :]
            for k in range(4):
                s = src[k * ROWS + 8 * g : k * ROWS + 8 * g + 8, window]
                top = jnp.max(s, axis=1, keepdims=True)
                p = jnp.exp2((s - top) * EXP_SCALE)
                total = total + p * (1.0 / jnp.sum(p, axis=1, keepdims=True))
            acc[rows, :] = total

    def relus(unit, dest):
        q4 = jnp.concatenate(
            [
                qbuf[unit // 4, pl.ds(pl.multiple_of(unit % 4 * ROWS, ROWS), ROWS), k * DI : (k + 1) * DI]
                for k in range(4)
            ],
            axis=0,
        )
        dest[:, 0:WIN] = jnp.dot(q4, ikt[:, window], preferred_element_type=F32)

    def score_sum(unit, src):
        mine = pltpu.roll(gates[...], lax.rem(ROWS - 4 * unit, ROWS), 1)
        for g in range(ROWS // 8):
            rows = slice(8 * g, 8 * g + 8)
            total = score[rows, :]
            for k in range(4):
                gate = mine[rows, k : k + 1]
                s = src[k * ROWS + 8 * g : k * ROWS + 8 * g + 8, 0:WIN]
                total = total + gate * jnp.maximum(s, 0.0)
            score[rows, :] = total

    heads_sum(rel_a.at[0])

    def mixed(i, last):
        relus(2 * i, rel_a.at[i])
        heads_sum(rel_b.at[i])
        relus(2 * i + 1, rel_b.at[i])
        score_sum(2 * i, rel_a.at[i])
        if not last:
            heads_sum(rel_a.at[i + 1])
        score_sum(2 * i + 1, rel_b.at[i])
        return 0

    lax.fori_loop(0, 7, lambda i, _: mixed(i, False), 0)
    mixed(7, True)

    factor = DI**-0.5
    key8 = seq * ROWS - LOOK + lax.broadcasted_iota(jnp.int32, (8, WIN), 1)
    row8 = seq * ROWS + lax.broadcasted_iota(jnp.int32, (8, WIN), 0)
    for g in range(ROWS // 8):
        rows = slice(8 * g, 8 * g + 8)
        start8 = jnp.concatenate([starts[rows, :]] * 9, axis=1)
        allowed = jnp.logical_and(key8 >= start8, key8 <= row8 + 8 * g)
        sc = jnp.where(allowed, score[rows, :] * factor, NEG)
        shifted = sc - jnp.max(sc, axis=1, keepdims=True)
        log_model = shifted - jnp.log(jnp.sum(jnp.exp(shifted), axis=1, keepdims=True))
        model = jnp.exp(log_model)
        target = acc[rows, :] * (1.0 / HEADS)
        positive = target > 0.0
        terms = jnp.where(positive, target * (jnp.log(jnp.where(positive, target, 1.0)) - log_model), 0.0)
        terms = jnp.where(allowed, terms, 0.0)
        divs[rows, :] = jnp.broadcast_to(jnp.sum(terms, axis=1, keepdims=True), (8, ROWS))
        dif[rows, :] = jnp.where(allowed, model - target, 0.0)
    div_ref[...] = divs[...].T[0:1, :]

    lane8 = lax.broadcasted_iota(jnp.int32, (8, ROWS), 1)

    def delta_sum(unit, src):
        for g in range(ROWS // 8):
            rows = slice(8 * g, 8 * g + 8)
            out = gd[rows, :]
            d8 = dif[rows, :]
            for k in range(4):
                s = src[k * ROWS + 8 * g : k * ROWS + 8 * g + 8, 0:WIN]
                value = jnp.sum(d8 * jnp.maximum(s, 0.0), axis=1, keepdims=True)
                out = jnp.where(lane8 == unit * 4 + k, value, out)
            gd[rows, :] = out

    def delta_step(i, _):
        delta_sum(2 * i, rel_a.at[i])
        delta_sum(2 * i + 1, rel_b.at[i])
        return 0

    lax.fori_loop(0, 8, delta_step, 0)
    delta = (gd[...] * factor / ROWS).astype(BF)
    gall[y] = delta
    g_copies = [remote(gall.at[y], gall.at[y], t_s.at[d], t_r.at[d], ys[d - 1]) for d in range(1, 4)]
    for c in g_copies:
        c.start()

    own_quarter.wait()
    for c in h_copies:
        c.wait()
    for j in range(4):
        for t in range(QUARTER // 128):
            ht[j, t * 128 : t * 128 + 128, :] = hy[j, :, t * 128 : t * 128 + 128].T
    for c in g_copies:
        c.wait()
    stack = []
    for j in range(4):
        wide = gall[j].astype(F32)
        stack += [wide, pltpu.roll(wide, 64, 1)]
    stack = jnp.concatenate(stack, axis=0).astype(BF)

    def part_step(i, _):
        lhs = jnp.concatenate(
            [
                ht[j, pl.ds(pl.multiple_of(i * 224 + c * 112, 16), 112), :]
                for j in range(4)
                for c in range(2)
            ],
            axis=1,
        )
        out = jnp.dot(lhs, stack, preferred_element_type=F32)
        pad = jnp.zeros((2, ROWS), F32)
        for xx in range(4):
            for half in range(2):
                at = xx * 28 + half * 14
                part[half, xx, i] = jnp.concatenate([out[at : at + 14, :], pad], axis=0)
        return 0

    lax.fori_loop(0, 8, part_step, 0)

    def exchange(copies):
        for c in copies:
            c.start()
        for c in copies:
            c.wait()

    exchange([remote(part.at[1 - core], rc, t_s.at[0], t_r.at[0], partner)])
    s1[...] = part[core] + rc[...]
    exchange([
        remote(s1.at[lax.rem(x + d, 4)], rx.at[d - 1], t_s.at[3 + d], t_r.at[3 + d], xs[d - 1])
        for d in range(1, 4)
    ])
    s2[...] = s1[x] + rx[0] + rx[1] + rx[2]
    exchange([
        remote(s2.at[lax.rem(z + d, 8)], rz.at[d - 1], t_s.at[6 + d], t_r.at[6 + d], zs[d - 1])
        for d in range(1, 8)
    ])
    total = s2[z]
    for d in range(7):
        total = total + rz[d]
    s3[...] = total
    exchange([remote(s3, fin, t_s.at[14], t_r.at[14], partner)])
    low = jnp.where(core == 0, s3[...], fin[...])
    high = jnp.where(core == 0, fin[...], s3[...])
    full = jnp.concatenate([low[0:14, :], high[0:14, :]], axis=0)
    out_ref[...] = jnp.where(core == 0, full[:, 0:64], full[:, 64:128])


def body(doc_lengths, hidden, gate_weight, target_query, latent_keys, index_query, index_keys):
    hbm = pl.BlockSpec(memory_space=pl.ANY)
    vmem = pl.BlockSpec(memory_space=pltpu.VMEM)
    dma = pltpu.SemaphoreType.DMA
    return pl.pallas_call(
        kernel,
        out_shape=(jax.ShapeDtypeStruct((1, ROWS), F32), jax.ShapeDtypeStruct((28, HEADS), F32)),
        in_specs=[pl.BlockSpec(memory_space=pltpu.SMEM)] + [hbm] * 5 + [vmem],
        out_specs=(vmem, vmem),
        scratch_shapes=[
            pltpu.VMEM((DEEP, 2 * ROWS), BF),
            pltpu.VMEM((DEEP, 2 * ROWS), BF),
            pltpu.VMEM((DI, PANEL), BF),
            pltpu.VMEM((SLOTS, UNIT, DEEP), BF),
            pltpu.VMEM((8, UNIT, PANEL), F32),
            pltpu.VMEM((8, UNIT, PANEL), F32),
            pltpu.VMEM((ROWS, WIN), F32),
            pltpu.VMEM((ROWS, WIN), F32),
            pltpu.VMEM((ROWS, WIN), F32),
            pltpu.VMEM((ROWS, ROWS), jnp.int32),
            pltpu.VMEM((ROWS, ROWS), F32),
            pltpu.VMEM((ROWS, ROWS), F32),
            pltpu.VMEM((ROWS, D), BF),
            pltpu.VMEM((10, LAT, ROWS), BF),
            pltpu.VMEM((PANEL, DI), BF),
            pltpu.VMEM((ROWS, ROWS), F32),
            pltpu.VMEM((4, 28, HEADS), BF),
            pltpu.VMEM((112, HEADS), F32),
            pltpu.VMEM((4, 8, 2, 112, HEADS), BF),
            pltpu.VMEM((4, ROWS, QUARTER), BF),
            pltpu.VMEM((4, QUARTER, ROWS), BF),
            pltpu.VMEM((4, ROWS, ROWS), BF),
            pltpu.VMEM((2, 4, 8, 16, ROWS), F32),
            pltpu.VMEM((4, 8, 16, ROWS), F32),
            pltpu.VMEM((4, 8, 16, ROWS), F32),
            pltpu.VMEM((3, 8, 16, ROWS), F32),
            pltpu.VMEM((8, 16, ROWS), F32),
            pltpu.VMEM((7, 16, ROWS), F32),
            pltpu.VMEM((16, ROWS), F32),
            pltpu.VMEM((16, ROWS), F32),
            dma((SLOTS, 4)), dma((5,)),
            dma((4, 2)), dma((4, 2)), dma((5, 2)), dma((5, 2)),
            dma((17,)), dma((17,)), dma((15,)), dma((15,)),
        ],
        compiler_params=pltpu.CompilerParams(
            collective_id=0, has_side_effects=True, vmem_limit_bytes=VMEM_MOST
        ),
    )(doc_lengths, target_query[0], index_query[0], hidden[0], latent_keys[0].T, index_keys[0], gate_weight)


def solution(mesh):
    split = Mesh(mesh.devices.reshape(4, 8, 2, mesh.shape["grp"]), SEQ_GRP)
    rows = P("grp", SEQ, None)
    in_specs = (P("grp", None), rows, P(SEQ_GRP, None), rows, rows, rows, rows)
    out_specs = (P("grp", SEQ), P(SEQ_GRP, None))
    return jax.shard_map(body, mesh=split, in_specs=in_specs, out_specs=out_specs, check_vma=False)
```

```python
import math

import jax
import jax.numpy as jnp
from jax import lax
from jax.experimental import pallas as pl
from jax.experimental.pallas import tpu as pltpu
from jax.sharding import Mesh
from jax.sharding import PartitionSpec as P

SEQ = ("seq_0", "seq_1", "seq_2")
SEQ_GRP = ("seq_0", "seq_1", "seq_2", "grp")
MESH = pl.DeviceIdType.MESH

ROWS = 128
HEADS = 64
LAT = 576
DI = 128
WIN = 1152
LOOK = 1024
D = 7168
DOCS = 16
PAIR = 2 * LAT
CUT = 640
DEEP = 768
PANEL = WIN + ROWS
QUARTER = D // 4
UNIT = 4 * ROWS
PASSES = ((6, 3), (2, 4), (0, 2))
SLOTS = 8
NEG = -1e30
TARGET_SCALE = 0.07216878364870322
EXP_SCALE = TARGET_SCALE * math.log2(math.e)
BF = jnp.bfloat16
F32 = jnp.float32
VMEM_MOST = 67_043_328


def sync_with(peers):
    barrier = pltpu.get_barrier_semaphore()
    for peer in peers:
        pl.semaphore_signal(barrier, inc=1, device_id=peer, device_id_type=MESH)
    pl.semaphore_wait(barrier, len(peers))


def chip_after(y, z):
    return {"seq_0": lax.rem(y + (z + 1) // 8, 4), "seq_1": lax.rem(z + 1, 8)}


def chip_before(y, z):
    return {"seq_0": lax.rem(y + 3 + (z + 7) // 8, 4), "seq_1": lax.rem(z + 7, 8)}


def kernel(
    lens_ref, q_hbm, iq_hbm, hid_hbm, lat_hbm, ik_hbm, gw_ref,
    div_ref, out_ref,
    ke, ko, ikt, qbuf, rel_a, rel_b, acc, score, dif, starts, divs, gates, hid, lat, ik, gd,
    wx, wcat, wb, hy, ht, gall, part, rc, s1, rx, s2, rz, s3, fin,
    qsem, isem, ring_s, ring_r, side_s, side_r, w_s, w_r, t_s, t_r,
):
    y, z, core, x = (lax.axis_index(a) for a in SEQ_GRP)
    chip = y * 8 + z
    seq = chip * 2 + core
    ahead, behind = chip_after(y, z), chip_before(y, z)
    partner = {"seq_2": 1 - core}
    xs = [{"grp": lax.rem(x + d, 4)} for d in range(1, 4)]
    ys = [{"seq_0": lax.rem(y + d, 4)} for d in range(1, 4)]
    zs = [{"seq_1": lax.rem(z + d, 8)} for d in range(1, 8)]

    def local(src, dst, sem):
        return pltpu.make_async_copy(src, dst, sem)

    def remote(src, dst, send, recv, peer):
        return pltpu.make_async_remote_copy(
            src_ref=src, dst_ref=dst, send_sem=send, recv_sem=recv, device_id=peer, device_id_type=MESH
        )

    def slot(k):
        return 8 - 2 * k + core

    def slot_rows(k):
        return pl.ds(pl.multiple_of((8 - 2 * k + core) * ROWS, ROWS), ROWS)

    def q_copy(unit, slot):
        quad, parity = unit // 2, unit % 2
        return [
            local(
                q_hbm.at[:, pl.ds(pl.multiple_of((quad * 4 + k) * PAIR + parity * (PAIR - CUT), 128), CUT)],
                qbuf.at[slot, pl.ds(k * ROWS, ROWS), pl.ds(0, CUT)],
                qsem.at[slot],
            )
            for k in range(4)
        ]

    def q_wait(slot):
        whole = qbuf.at[slot, :, pl.ds(0, CUT)]
        local(whole, whole, qsem.at[slot]).wait()

    own_lat = local(lat_hbm, lat.at[slot(0)], isem.at[0])
    own_ik = local(ik_hbm, ik.at[slot_rows(0)], isem.at[1])
    own_lat.start()
    own_ik.start()
    for u in range(SLOTS):
        for c in q_copy(u, u):
            c.start()
    sync_with([partner] + xs + ys + zs + [ahead, behind])

    def halves(k, own):
        lat_at, ik_at = (lat_hbm, ik_hbm) if own else (lat.at[slot(k)], ik.at[slot_rows(k)])
        half = LAT // 2
        return [[lat_at.at[pl.ds(0, half)]], [lat_at.at[pl.ds(half, half)], ik_at]]

    def ring(k, part):
        return [
            remote(a, b, ring_s.at[k, part + n], ring_r.at[k, part + n], ahead)
            for n, (a, b) in enumerate(zip(halves(k, k == 0)[part], halves(k + 1, False)[part]))
        ]

    def side(k, part):
        return [
            remote(a, b, side_s.at[k, part + n], side_r.at[k, part + n], partner)
            for n, (a, b) in enumerate(zip(halves(k, k == 0)[part], halves(k, False)[part]))
        ]

    hops = {}
    besides = []

    def start_from(k, part):
        if k < 4:
            hops[k + 1, part] = ring(k, part)
            for c in hops[k + 1, part]:
                c.start()
        pair = side(k, part)
        for c in pair:
            c.start()
        besides.extend(pair)

    def arrive(k, part):
        for c in hops[k, part]:
            c.wait()
        start_from(k, part)

    start_from(0, 0)
    start_from(0, 1)
    wx[x] = gw_ref[...]
    w_copies = [remote(gw_ref, wx.at[x], w_s.at[d], w_r.at[d], xs[d - 1]) for d in range(1, 4)]
    for c in w_copies:
        c.start()
    hid_in = local(hid_hbm, hid, isem.at[3])
    own_quarter = local(hid_hbm.at[:, pl.ds(pl.multiple_of(y * QUARTER, 128), QUARTER)], hy.at[y], isem.at[4])
    hid_in.start()
    own_quarter.start()

    row = lax.broadcasted_iota(jnp.int32, (ROWS, ROWS), 0)
    lane = lax.broadcasted_iota(jnp.int32, (ROWS, ROWS), 1)
    pos = seq * ROWS + row
    start = jnp.zeros((ROWS, ROWS), jnp.int32)
    end = jnp.int32(0)
    for k in range(DOCS):
        length = lens_ref[0, k]
        end = end + length
        start = start + jnp.where(pos >= end, length, 0)
    starts[...] = start
    eye = jnp.where(row == lane, 1.0, 0.0).astype(BF)
    for u in range(SLOTS):
        for k in range(4):
            qbuf[u, k * ROWS : (k + 1) * ROWS, CUT:DEEP] = eye
    ke[LAT:CUT, :] = jnp.zeros((CUT - LAT, 4 * ROWS), BF)
    ko[0 : CUT - LAT, :] = jnp.zeros((CUT - LAT, 4 * ROWS), BF)
    acc[...] = jnp.zeros((ROWS, WIN), F32)
    score[...] = jnp.zeros((ROWS, WIN), F32)
    gd[...] = jnp.zeros((ROWS, ROWS), F32)
    gates[...] = jnp.zeros((ROWS, ROWS), F32)
    own_lat.wait()
    own_ik.wait()

    def keys_of(first, count):
        for j in range(count):
            at = (first + j) * ROWS
            cols = slice(j * ROWS, (j + 1) * ROWS)
            key = seq * ROWS - LOOK + at + lane
            own_start = starts[...]
            bias = jnp.where(jnp.logical_and(key >= own_start, key <= pos), 0.0, NEG).astype(BF)
            ke[CUT:DEEP, cols] = bias
            ko[CUT:DEEP, cols] = bias
            block = lat[core + first + j]
            ke[0:LAT, cols] = block
            ko[CUT - LAT : CUT, cols] = block
            rows = pl.ds(pl.multiple_of((core + first + j) * ROWS, ROWS), ROWS)
            ikt[:, at : at + ROWS] = ik[rows, :].T

    def some_units(lo, hi, first, count, last):
        def units(i, _):
            for parity, keys, store in ((0, ke, rel_a), (1, ko, rel_b)):
                unit = 2 * i + parity
                slot = lax.rem(unit, SLOTS)
                q_wait(slot)
                store[i, :, first * ROWS : (first + count) * ROWS] = jnp.dot(
                    qbuf[slot], keys[:, 0 : count * ROWS], preferred_element_type=F32
                )
                if not last:
                    for c in q_copy(lax.rem(unit + SLOTS, 16), slot):
                        c.start()
                else:

                    @pl.when(unit + SLOTS < 16)
                    def _():
                        for c in q_copy(unit + SLOTS, slot):
                            c.start()

            return 0

        lax.fori_loop(lo, hi, units, 0)

    parts = [(k, part) for k in range(1, 5) for part in range(2)]
    for n, (first, count) in enumerate(PASSES):
        while parts and parts[0][0] <= (9 - first) // 2:
            arrive(*parts.pop(0))
        if n == 0:
            for c in w_copies:
                c.wait()
            for j in range(4):
                wcat[28 * j : 28 * j + 28, :] = wx[j].astype(F32)
            wb[y, z, core] = wcat[...].astype(BF)
            w_copies = [
                remote(wb.at[y, z, core], wb.at[y, z, core], w_s.at[3 + d], w_r.at[3 + d], zs[d - 1])
                for d in range(1, 8)
            ]
        if n == 1:
            for c in w_copies:
                c.wait()
            w_copies = [
                remote(wb.at[y, :, core], wb.at[y, :, core], w_s.at[10 + d], w_r.at[10 + d], ys[d - 1])
                for d in range(1, 4)
            ]
            h_copies = [
                remote(
                    hid_hbm.at[:, pl.ds(pl.multiple_of(lax.rem(y + d, 4) * QUARTER, 128), QUARTER)],
                    hy.at[y], w_s.at[13 + d], w_r.at[13 + d], ys[d - 1],
                )
                for d in range(1, 4)
            ]
        if n == 2:
            for c in w_copies:
                c.wait()
            w_copies = [remote(wb.at[:, :, core], wb.at[:, :, core], w_s.at[0], w_r.at[0], partner)]
        for c in w_copies:
            c.start()
        if n == 1:
            for c in h_copies:
                c.start()
        for c in besides:
            c.wait()
        besides.clear()
        keys_of(first, count)
        for quarter in range(4):
            some_units(2 * quarter, 2 * quarter + 2, first, count, n == len(PASSES) - 1)
            if quarter and parts:
                arrive(*parts.pop(0))

    iq_copies = [
        local(
            iq_hbm.at[:, pl.ds(u * 4 * DI, 4 * DI)],
            qbuf.at[u // 4, pl.ds(u % 4 * ROWS, ROWS), pl.ds(0, 4 * DI)],
            isem.at[5 + u],
        )
        for u in range(16)
    ]
    for c in iq_copies:
        c.start()
    for c in w_copies:
        c.wait()

    hid_in.wait()
    gates[:, 0:HEADS] = jnp.dot(hid[...], wb[...].reshape(D, HEADS), preferred_element_type=F32)
    for c in iq_copies:
        c.wait()

    def heads_sum(src):
        for g in range(ROWS // 8):
            rows = slice(8 * g, 8 * g + 8)
            total = acc[rows, :]
            for k in range(4):
                s = src[k * ROWS + 8 * g : k * ROWS + 8 * g + 8, :]
                top = jnp.max(s, axis=1, keepdims=True)
                p = jnp.exp2((s - top) * EXP_SCALE)
                total = total + p * (1.0 / jnp.sum(p, axis=1, keepdims=True))
            acc[rows, :] = total

    def relus(unit, dest):
        q4 = jnp.concatenate(
            [
                qbuf[unit // 4, pl.ds(pl.multiple_of(unit % 4 * ROWS, ROWS), ROWS), k * DI : (k + 1) * DI]
                for k in range(4)
            ],
            axis=0,
        )
        dest[...] = jnp.maximum(jnp.dot(q4, ikt[...], preferred_element_type=F32), 0.0)

    def score_sum(unit, src):
        mine = pltpu.roll(gates[...], lax.rem(ROWS - 4 * unit, ROWS), 1)
        for g in range(ROWS // 8):
            rows = slice(8 * g, 8 * g + 8)
            total = score[rows, :]
            for k in range(4):
                gate = mine[rows, k : k + 1]
                s = src[k * ROWS + 8 * g : k * ROWS + 8 * g + 8, :]
                total = total + gate * s
            score[rows, :] = total

    heads_sum(rel_a.at[0])

    def mixed(i, last):
        relus(2 * i, rel_a.at[i])
        heads_sum(rel_b.at[i])
        relus(2 * i + 1, rel_b.at[i])
        score_sum(2 * i, rel_a.at[i])
        if not last:
            heads_sum(rel_a.at[i + 1])
        score_sum(2 * i + 1, rel_b.at[i])
        return 0

    lax.fori_loop(0, 7, lambda i, _: mixed(i, False), 0)
    mixed(7, True)

    factor = DI**-0.5
    key8 = seq * ROWS - LOOK + lax.broadcasted_iota(jnp.int32, (8, WIN), 1)
    row8 = seq * ROWS + lax.broadcasted_iota(jnp.int32, (8, WIN), 0)
    for g in range(ROWS // 8):
        rows = slice(8 * g, 8 * g + 8)
        start8 = jnp.concatenate([starts[rows, :]] * 9, axis=1)
        allowed = jnp.logical_and(key8 >= start8, key8 <= row8 + 8 * g)
        sc = jnp.where(allowed, score[rows, :] * factor, NEG)
        shifted = sc - jnp.max(sc, axis=1, keepdims=True)
        log_model = shifted - jnp.log(jnp.sum(jnp.exp(shifted), axis=1, keepdims=True))
        model = jnp.exp(log_model)
        target = acc[rows, :] * (1.0 / HEADS)
        positive = target > 0.0
        terms = jnp.where(positive, target * (jnp.log(jnp.where(positive, target, 1.0)) - log_model), 0.0)
        terms = jnp.where(allowed, terms, 0.0)
        divs[rows, :] = jnp.broadcast_to(jnp.sum(terms, axis=1, keepdims=True), (8, ROWS))
        dif[rows, :] = jnp.where(allowed, model - target, 0.0)
    div_ref[...] = divs[...].T[0:1, :]

    lane8 = lax.broadcasted_iota(jnp.int32, (8, ROWS), 1)

    def delta_sum(unit, src):
        for g in range(ROWS // 8):
            rows = slice(8 * g, 8 * g + 8)
            out = gd[rows, :]
            d8 = dif[rows, :]
            for k in range(4):
                s = src[k * ROWS + 8 * g : k * ROWS + 8 * g + 8, :]
                value = jnp.sum(d8 * s, axis=1, keepdims=True)
                out = jnp.where(lane8 == unit * 4 + k, value, out)
            gd[rows, :] = out

    def delta_step(i, _):
        delta_sum(2 * i, rel_a.at[i])
        delta_sum(2 * i + 1, rel_b.at[i])
        return 0

    lax.fori_loop(0, 8, delta_step, 0)
    delta = (gd[...] * factor / ROWS).astype(BF)
    gall[y] = delta
    g_copies = [remote(gall.at[y], gall.at[y], t_s.at[d], t_r.at[d], ys[d - 1]) for d in range(1, 4)]
    for c in g_copies:
        c.start()

    own_quarter.wait()
    for c in h_copies:
        c.wait()
    for j in range(4):
        for t in range(QUARTER // 128):
            ht[j, t * 128 : t * 128 + 128, :] = hy[j, :, t * 128 : t * 128 + 128].T
    for c in g_copies:
        c.wait()
    stack = []
    for j in range(4):
        wide = gall[j].astype(F32)
        stack += [wide, pltpu.roll(wide, 64, 1)]
    stack = jnp.concatenate(stack, axis=0).astype(BF)

    def part_step(i, _):
        lhs = jnp.concatenate(
            [
                ht[j, pl.ds(pl.multiple_of(i * 224 + c * 112, 16), 112), :]
                for j in range(4)
                for c in range(2)
            ],
            axis=1,
        )
        out = jnp.dot(lhs, stack, preferred_element_type=F32)
        pad = jnp.zeros((2, ROWS), F32)
        for xx in range(4):
            for half in range(2):
                at = xx * 28 + half * 14
                part[half, xx, i] = jnp.concatenate([out[at : at + 14, :], pad], axis=0)
        return 0

    lax.fori_loop(0, 8, part_step, 0)

    def exchange(copies):
        for c in copies:
            c.start()
        for c in copies:
            c.wait()

    exchange([remote(part.at[1 - core], rc, t_s.at[0], t_r.at[0], partner)])
    s1[...] = part[core] + rc[...]
    exchange([
        remote(s1.at[lax.rem(x + d, 4)], rx.at[d - 1], t_s.at[3 + d], t_r.at[3 + d], xs[d - 1])
        for d in range(1, 4)
    ])
    s2[...] = s1[x] + rx[0] + rx[1] + rx[2]
    exchange([
        remote(s2.at[lax.rem(z + d, 8)], rz.at[d - 1], t_s.at[6 + d], t_r.at[6 + d], zs[d - 1])
        for d in range(1, 8)
    ])
    total = s2[z]
    for d in range(7):
        total = total + rz[d]
    s3[...] = total
    exchange([remote(s3, fin, t_s.at[14], t_r.at[14], partner)])
    low = jnp.where(core == 0, s3[...], fin[...])
    high = jnp.where(core == 0, fin[...], s3[...])
    full = jnp.concatenate([low[0:14, :], high[0:14, :]], axis=0)
    out_ref[...] = jnp.where(core == 0, full[:, 0:64], full[:, 64:128])


def body(doc_lengths, hidden, gate_weight, target_query, latent_keys, index_query, index_keys):
    hbm = pl.BlockSpec(memory_space=pl.ANY)
    vmem = pl.BlockSpec(memory_space=pltpu.VMEM)
    dma = pltpu.SemaphoreType.DMA
    return pl.pallas_call(
        kernel,
        out_shape=(jax.ShapeDtypeStruct((1, ROWS), F32), jax.ShapeDtypeStruct((28, HEADS), F32)),
        in_specs=[pl.BlockSpec(memory_space=pltpu.SMEM)] + [hbm] * 5 + [vmem],
        out_specs=(vmem, vmem),
        scratch_shapes=[
            pltpu.VMEM((DEEP, 4 * ROWS), BF),
            pltpu.VMEM((DEEP, 4 * ROWS), BF),
            pltpu.VMEM((DI, WIN), BF),
            pltpu.VMEM((SLOTS, UNIT, DEEP), BF),
            pltpu.VMEM((8, UNIT, WIN), F32),
            pltpu.VMEM((8, UNIT, WIN), F32),
            pltpu.VMEM((ROWS, WIN), F32),
            pltpu.VMEM((ROWS, WIN), F32),
            pltpu.VMEM((ROWS, WIN), F32),
            pltpu.VMEM((ROWS, ROWS), jnp.int32),
            pltpu.VMEM((ROWS, ROWS), F32),
            pltpu.VMEM((ROWS, ROWS), F32),
            pltpu.VMEM((ROWS, D), BF),
            pltpu.VMEM((10, LAT, ROWS), BF),
            pltpu.VMEM((PANEL, DI), BF),
            pltpu.VMEM((ROWS, ROWS), F32),
            pltpu.VMEM((4, 28, HEADS), BF),
            pltpu.VMEM((112, HEADS), F32),
            pltpu.VMEM((4, 8, 2, 112, HEADS), BF),
            pltpu.VMEM((4, ROWS, QUARTER), BF),
            pltpu.VMEM((4, QUARTER, ROWS), BF),
            pltpu.VMEM((4, ROWS, ROWS), BF),
            pltpu.VMEM((2, 4, 8, 16, ROWS), F32),
            pltpu.VMEM((4, 8, 16, ROWS), F32),
            pltpu.VMEM((4, 8, 16, ROWS), F32),
            pltpu.VMEM((3, 8, 16, ROWS), F32),
            pltpu.VMEM((8, 16, ROWS), F32),
            pltpu.VMEM((7, 16, ROWS), F32),
            pltpu.VMEM((16, ROWS), F32),
            pltpu.VMEM((16, ROWS), F32),
            dma((SLOTS,)), dma((21,)),
            dma((4, 3)), dma((4, 3)), dma((5, 3)), dma((5, 3)),
            dma((17,)), dma((17,)), dma((15,)), dma((15,)),
        ],
        compiler_params=pltpu.CompilerParams(
            collective_id=0, has_side_effects=True, vmem_limit_bytes=VMEM_MOST
        ),
    )(doc_lengths, target_query[0], index_query[0], hidden[0], latent_keys[0].T, index_keys[0], gate_weight)


def solution(mesh):
    split = Mesh(mesh.devices.reshape(4, 8, 2, mesh.shape["grp"]), SEQ_GRP)
    rows = P("grp", SEQ, None)
    in_specs = (P("grp", None), rows, P(SEQ_GRP, None), rows, rows, rows, rows)
    out_specs = (P("grp", SEQ), P(SEQ_GRP, None))
    return jax.shard_map(body, mesh=split, in_specs=in_specs, out_specs=out_specs, check_vma=False)
```
